32 devices in a mesh: tile: 16 (over z, y, x), level: 2 (over core).
Axes of the slice: x: 2, y: 2, z: 4, core: 2. Of those that a mesh axis runs over, the one named last changes fastest.
Arguments:
- anomalies: bfloat16 [512, 8, 2048], P(None, 'level', 'tile'), may hold values from -6 to 6
- footprint: bfloat16 [8192, 128], P('tile'), may hold values from -0.5 to 0.5
- weighting: float32 [8, 8192], P('level', 'tile'), may hold values from 0.02 to 0.3
- dual_rows: bfloat16 [8192, 512], P(('tile', 'level')), may hold values from -6 to 6
- taper_blocks: bfloat16 [4, 128, 512], replicated, may hold values from 0.099609375 to 1
- obs_count: int32 [16], replicated, may hold values from 1 to 512, 4096 in all
- near_tiles: int32 [16, 6], replicated, may hold values from 0 to 15, as said below
- taper_class: int32 [16, 6], P('tile'), may hold values from 0 to 3
Outputs:
- increment: float32 [512, 8, 2048], P(None, 'level', 'tile')
The draws below stay inside these ranges and needn't reach their ends.
Inputs may be any that keep to these rules, and one draw needn't show every extreme that they name: `near_tiles`: row t lists 6 different tiles, each within cyclic distance 4 of t, that is (t + d) mod 16 with |d| <= 4.
All inputs are finite; a program needn't handle non-finite values.
Results may differ from the reference program's by a relative error of at most 0.004.
Values may be sent and summed in bfloat16 or wider, within the bound.
A program may use at most 64 MiB of HBM per device.

```python
import math
import jax
import jax.numpy as jnp
import numpy as np
from jax import lax

M = 512
PTS = 128
OBS_CAP = 512
NB = 6
REACH = 4
CLASSES = 4
LEV = 8
NPTS = 2048
NOBS = 8192
N_TILE = 16


def draw_near_tiles(key, part):
    keys = jax.random.split(jax.random.fold_in(key, 17), N_TILE)

    def one_row(row_key):
        return jax.random.permutation(row_key, 2 * REACH + 1)[:NB]
    offsets = jax.vmap(one_row)(keys).astype(jnp.int32) - REACH
    base_ids = jnp.arange(N_TILE, dtype=jnp.int32)[:, None]
    return ((base_ids + offsets) % N_TILE).astype(jnp.int32)


def plant(array, key, low, largest):
    index_at = [jax.random.randint(jax.random.fold_in(key, axis), (), 0, length) for axis, length in enumerate(array.shape)]
    widest = array.shape.index(max(array.shape))
    next_to = index_at[:widest] + [(index_at[widest] + 1) % array.shape[widest]] + index_at[widest + 1:]
    return array.at[tuple(index_at)].set(low).at[tuple(next_to)].set(largest)


def block_scale(stream_key, dims, cuts, smallest, top_value):
    loudness, own = 1.0, jax.random.fold_in(stream_key, 6)
    for axis_at, blocks in cuts:
        draws = jnp.exp(jax.random.uniform(jax.random.fold_in(own, axis_at), (blocks,), jnp.float32, smallest / len(cuts), top_value / len(cuts)))
        loudness = loudness * jnp.repeat(draws, dims[axis_at] // blocks).reshape([-1 if axis == axis_at else 1 for axis in range(len(dims))])
    return loudness


def profile(number_of, total, limit, slope):
    weights = [(1 << 20) // math.isqrt(standing ** slope) + 1 for standing in range(2, number_of + 1)]
    surplus, counts = total - limit - (number_of - 1), [1] * (number_of - 1)
    while surplus > 0:
        movable = [i for i in range(number_of - 1) if counts[i] < limit]
        pool, remaining = sum([weights[i] for i in movable]), surplus
        for i in movable:
            more = min(limit - counts[i], max(1, remaining * weights[i] // pool), surplus)
            counts[i] = counts[i] + more
            surplus = surplus - more
    return np.array([limit] + counts)


def uneven(own_key, amount, total, reach, skew):
    if amount == 2:
        one = jax.random.randint(own_key, (), max(1, total - reach), min(reach, total - 1) + 1)
        return jnp.stack([one, total - one])
    tallies = jnp.asarray(profile(amount, total, reach, skew), jnp.int32)
    couples = (amount - 1) // 2
    source_of, taker = tallies[1:1 + 2 * couples:2], tallies[2:2 + 2 * couples:2]
    room = jnp.minimum(source_of - 1, reach - taker)
    passed = jax.random.randint(jax.random.fold_in(own_key, 1), (couples,), 0, 1 << 20) % (room + 1)
    tallies = tallies.at[1:1 + 2 * couples:2].set(source_of - passed).at[2:2 + 2 * couples:2].set(taker + passed)
    return tallies[jax.random.permutation(jax.random.fold_in(own_key, 2), amount)]


def centred(key, extent, spread, reach, cuts=(), kind=jnp.bfloat16):
    result = spread * jax.random.normal(key, extent, jnp.float32)
    if cuts:
        result = result * block_scale(key, extent, cuts, -0.22, 0.18)
    return jnp.clip(result, -reach, reach).astype(kind)


def setup_inputs(seed: int = 0) -> dict:
    key_list = jax.random.split(jax.random.key(seed), 9)
    anomalies = centred(key_list[0], (M, LEV, NPTS), 1.0, 6.0, ((1, 2), (2, 16)))
    footprint = centred(key_list[1], (NOBS, PTS), PTS ** -0.5, 0.5, ((0, 16),))
    weighting = jnp.clip(jnp.exp(math.log(0.3) - 2.7080503 * jax.random.uniform(key_list[2], (LEV, NOBS), jnp.float32) ** block_scale(key_list[2], (LEV, NOBS), ((0, 2), (1, 16)), -0.2, 0.2)), 0.02, 0.3)
    dual_rows = centred(key_list[3], (NOBS, M), 1.0, 6.0, ((0, 32),))
    taper_blocks = jnp.clip(jax.random.uniform(key_list[4], (CLASSES, PTS, OBS_CAP), jnp.float32, 0.099609375, 1.0), 0.099609375, 1.0).astype(jnp.bfloat16)
    obs_count = uneven(key_list[5], N_TILE, N_TILE * OBS_CAP // 2, OBS_CAP, 2).astype(jnp.int32)
    near_tiles = draw_near_tiles(jax.random.fold_in(key_list[8], 71), 0)
    taper_class = plant(jax.random.randint(key_list[7], (N_TILE, NB), 0, CLASSES), jax.random.fold_in(key_list[7], 1), 0, CLASSES - 1).astype(jnp.int32)
    return dict(anomalies=anomalies, footprint=footprint, weighting=weighting, dual_rows=dual_rows, taper_blocks=taper_blocks, obs_count=obs_count, near_tiles=near_tiles, taper_class=taper_class)


def reference(anomalies, footprint, weighting, dual_rows, taper_blocks, obs_count, near_tiles, taper_class):
    def observe(tile_num):
        state = lax.dynamic_slice_in_dim(anomalies, tile_num * PTS, PTS, 2).astype(jnp.float32)
        interp = lax.dynamic_slice_in_dim(footprint, tile_num * OBS_CAP, OBS_CAP, 0).astype(jnp.float32)
        vertical = lax.dynamic_slice_in_dim(weighting, tile_num * OBS_CAP, OBS_CAP, 1)
        projected = jnp.einsum('op,mlp->lom', interp, state)
        summed = jnp.einsum('lo,lom->om', vertical, projected)
        slot_ids = jnp.arange(OBS_CAP, dtype=jnp.int32)
        present = slot_ids < obs_count[tile_num]
        return jnp.where(present[:, None], summed, jnp.float32(0.0)).astype(jnp.bfloat16)

    tile_ids = jnp.arange(N_TILE, dtype=jnp.int32)
    observed = lax.map(observe, tile_ids)
    duals = dual_rows.reshape(N_TILE, OBS_CAP, M)

    def analyse(tile_num):
        state = lax.dynamic_slice_in_dim(anomalies, tile_num * PTS, PTS, 2)
        flat_state = state.reshape(M, LEV * PTS).astype(jnp.float32)
        running = jnp.zeros((M, LEV * PTS), jnp.float32)
        for which in range(NB):
            source = near_tiles[tile_num, which]
            rows_y = lax.dynamic_index_in_dim(observed, source, 0, keepdims=False).astype(jnp.float32)
            rows_w = lax.dynamic_index_in_dim(duals, source, 0, keepdims=False).astype(jnp.float32)
            taper = lax.dynamic_index_in_dim(taper_blocks, taper_class[tile_num, which], 0, keepdims=False).astype(jnp.float32)
            covar = jnp.dot(flat_state.T, rows_y.T, preferred_element_type=jnp.float32)
            scaled = taper / jnp.float32(M - 1)
            tapered = (covar.reshape(LEV, PTS, OBS_CAP) * scaled[None]).reshape(LEV * PTS, OBS_CAP).astype(jnp.bfloat16)
            running = running + jnp.dot(rows_w.T, tapered.astype(jnp.float32).T, preferred_element_type=jnp.float32)
        return running.reshape(M, LEV, PTS)

    pieces = lax.map(analyse, tile_ids)
    return jnp.transpose(pieces, (1, 2, 0, 3)).reshape(M, LEV, NPTS)
```

```python
import functools
import jax
import jax.numpy as jnp
from jax import lax
from jax.experimental import pallas as pl
from jax.experimental.pallas import tpu as pltpu
from jax.sharding import PartitionSpec as P

MESH = pl.DeviceIdType.MESH
PLANE = 4
SLOTS = 9
W, Y = 0, 1


def kernel(
    tiles, levels, near_count,
    counts_ref, near_ref, class_ref, state_ref, foot_ref, weight_ref, dual_ref, taper_ref,
    out_ref,
    w_buf, y_buf, sums, others, ici_send, ici_recv, sib_send, sib_recv, part_send, part_recv,
):
    t = lax.axis_index("tile")
    l = lax.axis_index("level")
    owned, members = dual_ref.shape
    cells = state_ref.shape[0]
    points = foot_ref.shape[1]
    lev_dev = cells // points
    p = lax.rem(t, PLANE)
    base = t - p
    odd_x = lax.rem(p, 2)
    odd_y = p // 2
    xn = t + 1 - 2 * odd_x
    yn = t + 2 - 4 * odd_y
    zp = lax.rem(t + PLANE, tiles)
    zm = lax.rem(t + tiles - PLANE, tiles)
    low = lax.rem(base + tiles - PLANE, tiles)
    high = lax.rem(base + PLANE, tiles)
    uneven = lax.rem(odd_x + odd_y, 2)
    bufs = (w_buf, y_buf)

    def sibling(k):
        return lax.rem(l + k, levels)

    barrier = pltpu.get_barrier_semaphore()
    for other in (xn, yn, zp, zm):
        pl.semaphore_signal(barrier, inc=1, device_id=(other, l), device_id_type=MESH)
    for k in range(1, levels):
        pl.semaphore_signal(barrier, inc=1, device_id=(t, sibling(k)), device_id_type=MESH)
    pl.semaphore_wait(barrier, 3 + levels)

    started = []
    ici = {}
    sib = {}

    def rows(a, slot):
        return bufs[a].at[slot, pl.ds(pl.multiple_of(l * owned, owned), owned)]

    def send(a, src, slot, to):
        copy = pltpu.make_async_remote_copy(
            src_ref=src,
            dst_ref=rows(a, slot),
            send_sem=ici_send.at[a, slot - 1],
            recv_sem=ici_recv.at[a, slot - 1],
            device_id=(to, l),
            device_id_type=MESH,
        )
        copy.start()
        started.append(copy)
        ici[a, slot] = copy

    def share(a, slot, src=None):
        for k in range(1, levels):
            copy = pltpu.make_async_remote_copy(
                src_ref=rows(a, slot) if src is None else src,
                dst_ref=rows(a, slot),
                send_sem=sib_send.at[a, slot, k - 1],
                recv_sem=sib_recv.at[a, slot, k - 1],
                device_id=(t, sibling(k)),
                device_id_type=MESH,
            )
            copy.start()
            started.append(copy)
            sib[a, slot, k] = copy

    def arrive(a, slot):
        ici[a, slot].wait_recv()
        return None

    def together(slot):
        for a in (W, Y):
            for k in range(1, levels):
                sib[a, slot, k].wait_recv()

    send(W, dual_ref, 4, zp)
    send(W, dual_ref, 5, zm)
    send(W, dual_ref, 1, xn)
    send(W, dual_ref, 2, yn)
    share(W, 0, dual_ref)

    def part(who):
        first = pl.multiple_of(who * owned, owned)
        feet = foot_ref[pl.ds(first, owned), :]
        total = None
        for j in range(lev_dev):
            seen = jnp.dot(
                feet,
                state_ref[j * points : (j + 1) * points, :],
                preferred_element_type=jnp.float32,
            )
            seen = weight_ref[pl.ds(first, owned), j : j + 1] * seen
            total = seen if total is None else total + seen
        return total

    parts = []
    for k in range(1, levels):
        sums[k - 1] = part(sibling(k))
        copy = pltpu.make_async_remote_copy(
            src_ref=sums.at[k - 1],
            dst_ref=others.at[k - 1],
            send_sem=part_send.at[k - 1],
            recv_sem=part_recv.at[k - 1],
            device_id=(t, sibling(k)),
            device_id_type=MESH,
        )
        copy.start()
        started.append(copy)
        parts.append(copy)
    observed = part(l)
    for k, copy in enumerate(parts):
        copy.wait_recv()
        observed = observed + others[k]
    slot_ids = l * owned + lax.broadcasted_iota(jnp.int32, observed.shape, 0)
    own = pl.ds(pl.multiple_of(l * owned, owned), owned)
    y_buf[0, own, :] = jnp.where(slot_ids < counts_ref[t], observed, 0.0).astype(jnp.bfloat16)
    send(Y, rows(Y, 0), 4, zp)
    send(Y, rows(Y, 0), 5, zm)
    send(Y, rows(Y, 0), 1, xn)
    send(Y, rows(Y, 0), 2, yn)
    share(Y, 0)
    w_buf[0, own, :] = dual_ref[...]

    def near_of(lower, position):
        return jnp.where(lower == 1, low, high) + position

    tile_of = [
        t, xn, yn, base + PLANE - 1 - p, zm, zp,
        near_of(1 - odd_x, xn - base),
        near_of(1 - odd_y, yn - base),
        near_of(1 - odd_y, PLANE - 1 - p),
    ]

    def compute(slot, first=False):
        listed = jnp.int32(0)
        which = jnp.int32(0)
        for k in range(near_count):
            hit = jnp.where(near_ref[t, k] == tile_of[slot], 1, 0)
            listed = listed + hit
            which = which + hit * class_ref[0, k]
        scaled = taper_ref[which].astype(jnp.float32) / jnp.float32(members - 1)
        scaled = scaled * listed.astype(jnp.float32)
        covar = lax.dot_general(
            state_ref[...],
            y_buf[slot],
            (((1,), (1,)), ((), ())),
            preferred_element_type=jnp.float32,
        )
        tapered = (
            (covar.reshape(lev_dev, points, covar.shape[1]) * scaled[None])
            .reshape(covar.shape)
            .astype(jnp.bfloat16)
        )
        gain = jnp.dot(tapered, w_buf[slot], preferred_element_type=jnp.float32)
        out_ref[...] = gain if first else out_ref[...] + gain

    def relay_plane(a):
        src = rows(a, 1 + uneven)
        send(a, src, 3, jnp.where(uneven == 1, xn, yn))

    def spread(a):
        send(a, rows(a, 5 - odd_x), 6, xn)
        send(a, rows(a, 5 - odd_y), 7, yn)

    def relay_far(a):
        src = rows(a, 7 - uneven)
        send(a, src, 8, jnp.where(uneven == 1, yn, xn))

    together(0)
    compute(0, True)
    arrive(W, 1)
    arrive(W, 2)
    relay_plane(W)
    share(W, 1)
    share(W, 2)
    arrive(W, 4)
    arrive(W, 5)
    spread(W)
    share(W, 4)
    share(W, 5)
    arrive(Y, 1)
    arrive(Y, 2)
    relay_plane(Y)
    share(Y, 1)
    share(Y, 2)
    together(1)
    compute(1)
    together(2)
    compute(2)
    arrive(W, 3)
    share(W, 3)
    arrive(W, 6)
    arrive(W, 7)
    relay_far(W)
    share(W, 6)
    share(W, 7)
    arrive(Y, 4)
    arrive(Y, 5)
    spread(Y)
    share(Y, 4)
    share(Y, 5)
    arrive(Y, 3)
    share(Y, 3)
    together(3)
    compute(3)
    together(4)
    compute(4)
    together(5)
    compute(5)
    arrive(Y, 6)
    arrive(Y, 7)
    relay_far(Y)
    share(Y, 6)
    share(Y, 7)
    together(6)
    compute(6)
    together(7)
    compute(7)
    arrive(W, 8)
    share(W, 8)
    arrive(Y, 8)
    share(Y, 8)
    together(8)
    compute(8)
    for copy in started:
        copy.wait_send()


def shards(
    tiles, levels,
    anomalies, footprint, weighting, dual_rows, taper_blocks, obs_count, near_tiles, taper_class
):
    members, lev_dev, points = anomalies.shape
    owned = dual_rows.shape[0]
    cells = lev_dev * points
    state = anomalies.transpose(1, 2, 0).reshape(cells, members)
    smem = pl.BlockSpec(memory_space=pltpu.SMEM)
    vmem = pl.BlockSpec(memory_space=pltpu.VMEM)
    out = pl.pallas_call(
        functools.partial(kernel, tiles, levels, near_tiles.shape[1]),
        out_shape=jax.ShapeDtypeStruct((cells, members), jnp.float32),
        in_specs=[smem] * 3 + [vmem] * 5,
        out_specs=vmem,
        scratch_shapes=[
            pltpu.VMEM((SLOTS, levels * owned, members), jnp.bfloat16),
            pltpu.VMEM((SLOTS, levels * owned, members), jnp.bfloat16),
            pltpu.VMEM((levels - 1, owned, members), jnp.float32),
            pltpu.VMEM((levels - 1, owned, members), jnp.float32),
            pltpu.SemaphoreType.DMA((2, SLOTS - 1)),
            pltpu.SemaphoreType.DMA((2, SLOTS - 1)),
            pltpu.SemaphoreType.DMA((2, SLOTS, levels - 1)),
            pltpu.SemaphoreType.DMA((2, SLOTS, levels - 1)),
            pltpu.SemaphoreType.DMA((levels - 1,)),
            pltpu.SemaphoreType.DMA((levels - 1,)),
        ],
        compiler_params=pltpu.CompilerParams(
            collective_id=0, has_side_effects=True, vmem_limit_bytes=48 * 1024 * 1024
        ),
    )(obs_count, near_tiles, taper_class, state, footprint, weighting.T, dual_rows, taper_blocks)
    return out.T.reshape(members, lev_dev, points)


def solution(mesh):
    return jax.shard_map(
        functools.partial(shards, mesh.shape["tile"], mesh.shape["level"]),
        mesh=mesh,
        in_specs=(
            P(None, "level", "tile"),
            P("tile", None),
            P("level", "tile"),
            P(("tile", "level"), None),
            P(),
            P(),
            P(),
            P("tile", None),
        ),
        out_specs=P(None, "level", "tile"),
        check_vma=False,
    )
```

```python
import functools
import jax
import jax.numpy as jnp
from jax import lax
from jax.experimental import pallas as pl
from jax.experimental.pallas import tpu as pltpu
from jax.sharding import PartitionSpec as P

MESH = pl.DeviceIdType.MESH
PLANE = 4
SLOTS = 9
W, Y = 0, 1


def kernel(
    tiles, levels, near_count,
    counts_ref, near_ref, class_ref, state_ref, foot_ref, weight_ref, dual_ref, taper_ref,
    out_ref,
    w_buf, y_buf, sums, others, ici_send, ici_recv, sib_send, sib_recv, part_send, part_recv,
):
    t = lax.axis_index("tile")
    l = lax.axis_index("level")
    owned, members = dual_ref.shape
    chunks = w_buf.shape[1]
    chunk = owned // chunks
    cells = state_ref.shape[0]
    points = foot_ref.shape[1]
    lev_dev = cells // points
    p = lax.rem(t, PLANE)
    base = t - p
    odd_x = lax.rem(p, 2)
    odd_y = p // 2
    xn = t + 1 - 2 * odd_x
    yn = t + 2 - 4 * odd_y
    zp = lax.rem(t + PLANE, tiles)
    zm = lax.rem(t + tiles - PLANE, tiles)
    low = lax.rem(base + tiles - PLANE, tiles)
    high = lax.rem(base + PLANE, tiles)
    uneven = lax.rem(odd_x + odd_y, 2)
    bufs = (w_buf, y_buf)

    def sibling(k):
        return lax.rem(l + k, levels)

    barrier = pltpu.get_barrier_semaphore()
    for other in (xn, yn, zp, zm):
        pl.semaphore_signal(barrier, inc=1, device_id=(other, l), device_id_type=MESH)
    for k in range(1, levels):
        pl.semaphore_signal(barrier, inc=1, device_id=(t, sibling(k)), device_id_type=MESH)
    pl.semaphore_wait(barrier, 3 + levels)

    started = []

    def rows(a, slot, h):
        return bufs[a].at[slot, h, pl.ds(pl.multiple_of(l * chunk, chunk), chunk)]

    def hop(a, src, slot, h, to):
        return pltpu.make_async_remote_copy(
            src_ref=src,
            dst_ref=rows(a, slot, h),
            send_sem=ici_send.at[a, slot - 1, h],
            recv_sem=ici_recv.at[a, slot - 1, h],
            device_id=(to, l),
            device_id_type=MESH,
        )

    def send(a, src, slot, h, to):
        copy = hop(a, src, slot, h, to)
        copy.start()
        started.append(copy)

    def across(a, slot, h, k, src=None):
        return pltpu.make_async_remote_copy(
            src_ref=rows(a, slot, h) if src is None else src,
            dst_ref=rows(a, slot, h),
            send_sem=sib_send.at[a, slot, h, k - 1],
            recv_sem=sib_recv.at[a, slot, h, k - 1],
            device_id=(t, sibling(k)),
            device_id_type=MESH,
        )

    def share(a, slot, h, src=None):
        for k in range(1, levels):
            copy = across(a, slot, h, k, src)
            copy.start()
            started.append(copy)

    def arrive(a, h, *slots):
        for slot in slots:
            hop(a, rows(a, slot, h), slot, h, xn).wait_recv()

    def together(slot, h):
        for a in (W, Y):
            for k in range(1, levels):
                across(a, slot, h, k).wait_recv()

    def dual(h):
        return dual_ref.at[h * chunk : (h + 1) * chunk]

    for h in range(chunks):
        send(W, dual(h), 4, h, zp)
        send(W, dual(h), 5, h, zm)
        send(W, dual(h), 1, h, xn)
        send(W, dual(h), 2, h, yn)
    for h in range(chunks):
        share(W, 0, h, dual(h))

    def part(who):
        first = pl.multiple_of(who * owned, owned)
        feet = foot_ref[pl.ds(first, owned), :]
        total = None
        for j in range(lev_dev):
            seen = jnp.dot(
                feet,
                state_ref[j * points : (j + 1) * points, :],
                preferred_element_type=jnp.float32,
            )
            seen = weight_ref[pl.ds(first, owned), j : j + 1] * seen
            total = seen if total is None else total + seen
        return total

    parts = []
    for k in range(1, levels):
        sums[k - 1] = part(sibling(k))
        copy = pltpu.make_async_remote_copy(
            src_ref=sums.at[k - 1],
            dst_ref=others.at[k - 1],
            send_sem=part_send.at[k - 1],
            recv_sem=part_recv.at[k - 1],
            device_id=(t, sibling(k)),
            device_id_type=MESH,
        )
        copy.start()
        started.append(copy)
        parts.append(copy)
    observed = part(l)
    for k, copy in enumerate(parts):
        copy.wait_recv()
        observed = observed + others[k]
    slot_ids = l * owned + lax.broadcasted_iota(jnp.int32, observed.shape, 0)
    observed = jnp.where(slot_ids < counts_ref[t], observed, 0.0).astype(jnp.bfloat16)
    own = pl.ds(pl.multiple_of(l * chunk, chunk), chunk)
    for h in range(chunks):
        y_buf[0, h, own, :] = observed[h * chunk : (h + 1) * chunk]
    for h in range(chunks):
        send(Y, rows(Y, 0, h), 4, h, zp)
        send(Y, rows(Y, 0, h), 5, h, zm)
        send(Y, rows(Y, 0, h), 1, h, xn)
        send(Y, rows(Y, 0, h), 2, h, yn)
    for h in range(chunks):
        share(Y, 0, h)
        w_buf[0, h, own, :] = dual_ref[h * chunk : (h + 1) * chunk, :]

    def near_of(lower, position):
        return jnp.where(lower == 1, low, high) + position

    ahead_x = near_of(1 - odd_x, xn - base)
    ahead_y = near_of(1 - odd_y, yn - base)
    relayed, final = 7 - uneven, 6 + uneven
    tile_of = (
        (0, t), (1, xn), (2, yn), (3, base + PLANE - 1 - p), (4, zm), (5, zp),
        (relayed, jnp.where(uneven == 1, ahead_x, ahead_y)),
        (final, jnp.where(uneven == 1, ahead_y, ahead_x)),
        (8, near_of(1 - odd_y, PLANE - 1 - p)),
    )

    def compute(slot, h, first=False):
        together(slot, h)
        tile = [its for where, its in tile_of if where is slot][0]
        listed = jnp.int32(0)
        which = jnp.int32(0)
        for k in range(near_count):
            hit = jnp.where(near_ref[k, t] == tile, 1, 0)
            listed = listed + hit
            which = which + hit * class_ref[0, k]
        scaled = taper_ref[which]
        if chunks > 1:
            scaled = jnp.concatenate(
                [
                    scaled[:, who * owned + h * chunk : who * owned + (h + 1) * chunk]
                    for who in range(levels)
                ],
                axis=1,
            )
        scaled = scaled.astype(jnp.float32) / jnp.float32(members - 1)
        scaled = scaled * listed.astype(jnp.float32)
        covar = lax.dot_general(
            state_ref[...],
            y_buf[slot, h],
            (((1,), (1,)), ((), ())),
            preferred_element_type=jnp.float32,
        )
        tapered = (
            (covar.reshape(lev_dev, points, covar.shape[1]) * scaled[None])
            .reshape(covar.shape)
            .astype(jnp.bfloat16)
        )
        gain = jnp.dot(tapered, w_buf[slot, h], preferred_element_type=jnp.float32)
        out_ref[...] = gain if first else out_ref[...] + gain

    def relay_plane(a, h):
        send(a, rows(a, 1 + uneven, h), 3, h, jnp.where(uneven == 1, xn, yn))
        share(a, 1, h)
        share(a, 2, h)

    def spread(a, h):
        send(a, rows(a, 5 - odd_x, h), 6, h, xn)
        send(a, rows(a, 5 - odd_y, h), 7, h, yn)
        share(a, 4, h)
        share(a, 5, h)

    def relay_far(a, h):
        send(a, rows(a, relayed, h), 8, h, jnp.where(uneven == 1, yn, xn))
        share(a, relayed, h)

    every = range(chunks)
    last = chunks - 1
    arrive(W, 0, 1, 2)
    relay_plane(W, 0)
    compute(0, 0, True)
    arrive(W, 0, 4, 5)
    spread(W, 0)
    for h in range(1, chunks):
        arrive(W, h, 1, 2)
        relay_plane(W, h)
        compute(0, h)
    arrive(Y, 0, 1, 2)
    relay_plane(Y, 0)
    for h in range(1, chunks):
        arrive(W, h, 4, 5)
        spread(W, h)
        arrive(Y, h, 1, 2)
        relay_plane(Y, h)
    for h in every:
        compute(1, h)
        compute(2, h)
    arrive(W, 0, relayed)
    relay_far(W, 0)
    arrive(Y, 0, 4, 5)
    spread(Y, 0)
    for h in range(1, chunks):
        arrive(W, h, relayed)
        relay_far(W, h)
    compute(4, 0)
    compute(5, 0)
    for h in range(1, chunks):
        arrive(Y, h, 4, 5)
        spread(Y, h)
    arrive(Y, 0, relayed)
    relay_far(Y, 0)
    for h in range(1, chunks):
        compute(4, h)
        compute(5, h)
    for h in every:
        for a in (W, Y):
            arrive(a, h, 3)
            share(a, 3, h)
    compute(3, 0)
    compute(relayed, 0)
    for h in range(1, chunks):
        arrive(Y, h, relayed)
        relay_far(Y, h)
        compute(3, h)
    for h in every:
        arrive(W, h, final)
        share(W, final, h)
        arrive(W, h, 8)
        share(W, 8, h)
    for h in range(1, chunks):
        compute(relayed, h)
    for h in every:
        for slot in (final, 8):
            arrive(Y, h, slot)
            share(Y, slot, h)
            if h < last:
                compute(slot, h)
    compute(final, last)
    compute(8, last)
    for copy in started:
        copy.wait_send()


def shards(
    tiles, levels,
    anomalies, footprint, weighting, dual_rows, taper_blocks, obs_count, near_tiles, taper_class
):
    members, lev_dev, points = anomalies.shape
    owned = dual_rows.shape[0]
    cells = lev_dev * points
    chunks = max(1, owned // points)
    state = anomalies.transpose(1, 2, 0).reshape(cells, members)
    smem = pl.BlockSpec(memory_space=pltpu.SMEM)
    vmem = pl.BlockSpec(memory_space=pltpu.VMEM)
    out = pl.pallas_call(
        functools.partial(kernel, tiles, levels, near_tiles.shape[1]),
        out_shape=jax.ShapeDtypeStruct((cells, members), jnp.float32),
        in_specs=[smem] * 3 + [vmem] * 5,
        out_specs=vmem,
        scratch_shapes=[
            pltpu.VMEM((SLOTS, chunks, levels * owned // chunks, members), jnp.bfloat16),
            pltpu.VMEM((SLOTS, chunks, levels * owned // chunks, members), jnp.bfloat16),
            pltpu.VMEM((levels - 1, owned, members), jnp.float32),
            pltpu.VMEM((levels - 1, owned, members), jnp.float32),
            pltpu.SemaphoreType.DMA((2, SLOTS - 1, chunks)),
            pltpu.SemaphoreType.DMA((2, SLOTS - 1, chunks)),
            pltpu.SemaphoreType.DMA((2, SLOTS, chunks, levels - 1)),
            pltpu.SemaphoreType.DMA((2, SLOTS, chunks, levels - 1)),
            pltpu.SemaphoreType.DMA((levels - 1,)),
            pltpu.SemaphoreType.DMA((levels - 1,)),
        ],
        compiler_params=pltpu.CompilerParams(
            collective_id=0, has_side_effects=True, vmem_limit_bytes=48 * 1024 * 1024
        ),
    )(obs_count, near_tiles.T, taper_class, state, footprint, weighting.T, dual_rows, taper_blocks)
    return out.T.reshape(members, lev_dev, points)


def solution(mesh):
    return jax.shard_map(
        functools.partial(shards, mesh.shape["tile"], mesh.shape["level"]),
        mesh=mesh,
        in_specs=(
            P(None, "level", "tile"),
            P("tile", None),
            P("level", "tile"),
            P(("tile", "level"), None),
            P(),
            P(),
            P(),
            P("tile", None),
        ),
        out_specs=P(None, "level", "tile"),
        check_vma=False,
    )
```

```python
import functools
import jax
import jax.numpy as jnp
from jax import lax
from jax.experimental import pallas as pl
from jax.experimental.pallas import tpu as pltpu
from jax.sharding import PartitionSpec as P

MESH = pl.DeviceIdType.MESH
PLANE = 4
SLOTS = 9
CHUNK = 64
W, Y = 0, 1


def kernel(
    tiles, levels, near_count,
    counts_ref, near_ref, class_ref, raw_ref, foot_ref, weight_ref, dual_ref, taper_ref,
    out_ref,
    state_ref, w_buf, y_buf, sums, others, ici_send, ici_recv, sib_send, sib_recv, part_send, part_recv,
):
    t = lax.axis_index("tile")
    l = lax.axis_index("level")
    owned, members = dual_ref.shape
    halves = w_buf.shape[1]
    half = owned // halves
    subs = max(1, half // CHUNK)
    chunk = half // subs
    chunks = halves * subs
    cells = state_ref.shape[0]
    points = foot_ref.shape[1]
    lev_dev = cells // points
    p = lax.rem(t, PLANE)
    base = t - p
    odd_x = lax.rem(p, 2)
    odd_y = p // 2
    xn = t + 1 - 2 * odd_x
    yn = t + 2 - 4 * odd_y
    zp = lax.rem(t + PLANE, tiles)
    zm = lax.rem(t + tiles - PLANE, tiles)
    low = lax.rem(base + tiles - PLANE, tiles)
    high = lax.rem(base + PLANE, tiles)
    uneven = lax.rem(odd_x + odd_y, 2)
    bufs = (w_buf, y_buf)

    def sibling(k):
        return lax.rem(l + k, levels)

    barrier = pltpu.get_barrier_semaphore()
    for other in (xn, yn, zp, zm):
        pl.semaphore_signal(barrier, inc=1, device_id=(other, l), device_id_type=MESH)
    for k in range(1, levels):
        pl.semaphore_signal(barrier, inc=1, device_id=(t, sibling(k)), device_id_type=MESH)
    pl.semaphore_wait(barrier, 3 + levels)

    started = []

    def rows(a, slot, h):
        first = l * half + (h % subs) * chunk
        return bufs[a].at[slot, h // subs, pl.ds(pl.multiple_of(first, chunk), chunk)]

    def hop(a, src, slot, h, to):
        return pltpu.make_async_remote_copy(
            src_ref=src,
            dst_ref=rows(a, slot, h),
            send_sem=ici_send.at[a, slot - 1, h],
            recv_sem=ici_recv.at[a, slot - 1, h],
            device_id=(to, l),
            device_id_type=MESH,
        )

    def send(a, src, slot, h, to):
        copy = hop(a, src, slot, h, to)
        copy.start()
        started.append(copy)

    def across(a, slot, h, k, src=None):
        return pltpu.make_async_remote_copy(
            src_ref=rows(a, slot, h) if src is None else src,
            dst_ref=rows(a, slot, h),
            send_sem=sib_send.at[a, slot, h, k - 1],
            recv_sem=sib_recv.at[a, slot, h, k - 1],
            device_id=(t, sibling(k)),
            device_id_type=MESH,
        )

    def share(a, slot, h, src=None):
        for k in range(1, levels):
            copy = across(a, slot, h, k, src)
            copy.start()
            started.append(copy)

    def arrive(a, h, *slots):
        for slot in slots:
            hop(a, rows(a, slot, h), slot, h, xn).wait_recv()

    def together(slot, h):
        for a in (W, Y):
            for k in range(1, levels):
                across(a, slot, h, k).wait_recv()

    def dual(h):
        return dual_ref.at[h * chunk : (h + 1) * chunk]

    for h in range(chunks):
        send(W, dual(h), 4, h, zp)
        send(W, dual(h), 5, h, zm)
        send(W, dual(h), 1, h, xn)
        send(W, dual(h), 2, h, yn)
    for h in range(chunks):
        share(W, 0, h, dual(h))

    for j in range(lev_dev):
        state_ref[j * points : (j + 1) * points, :] = raw_ref[:, j, :].T

    def part(who):
        first = pl.multiple_of(who * owned, owned)
        feet = foot_ref[pl.ds(first, owned), :]
        total = None
        for j in range(lev_dev):
            seen = jnp.dot(
                feet,
                state_ref[j * points : (j + 1) * points, :],
                preferred_element_type=jnp.float32,
            )
            seen = weight_ref[pl.ds(first, owned), j : j + 1] * seen
            total = seen if total is None else total + seen
        return total

    parts = []
    for k in range(1, levels):
        sums[k - 1] = part(sibling(k))
        copy = pltpu.make_async_remote_copy(
            src_ref=sums.at[k - 1],
            dst_ref=others.at[k - 1],
            send_sem=part_send.at[k - 1],
            recv_sem=part_recv.at[k - 1],
            device_id=(t, sibling(k)),
            device_id_type=MESH,
        )
        copy.start()
        started.append(copy)
        parts.append(copy)
    observed = part(l)
    for k, copy in enumerate(parts):
        copy.wait_recv()
        observed = observed + others[k]
    slot_ids = l * owned + lax.broadcasted_iota(jnp.int32, observed.shape, 0)
    observed = jnp.where(slot_ids < counts_ref[t], observed, 0.0).astype(jnp.bfloat16)
    own = pl.ds(pl.multiple_of(l * half, half), half)
    for c in range(halves):
        y_buf[0, c, own, :] = observed[c * half : (c + 1) * half]
    for h in range(chunks):
        send(Y, rows(Y, 0, h), 4, h, zp)
        send(Y, rows(Y, 0, h), 5, h, zm)
        send(Y, rows(Y, 0, h), 1, h, xn)
        send(Y, rows(Y, 0, h), 2, h, yn)
    for h in range(chunks):
        share(Y, 0, h)
    for c in range(halves):
        w_buf[0, c, own, :] = dual_ref[c * half : (c + 1) * half, :]

    def near_of(lower, position):
        return jnp.where(lower == 1, low, high) + position

    ahead_x = near_of(1 - odd_x, xn - base)
    ahead_y = near_of(1 - odd_y, yn - base)
    relayed, final = 7 - uneven, 6 + uneven
    tile_of = (
        (0, t), (1, xn), (2, yn), (3, base + PLANE - 1 - p), (4, zm), (5, zp),
        (relayed, jnp.where(uneven == 1, ahead_x, ahead_y)),
        (final, jnp.where(uneven == 1, ahead_y, ahead_x)),
        (8, near_of(1 - odd_y, PLANE - 1 - p)),
    )

    def compute(slot, c, first=False):
        for h in range(c * subs, (c + 1) * subs):
            together(slot, h)
        tile = [its for where, its in tile_of if where is slot][0]
        listed = jnp.int32(0)
        which = jnp.int32(0)
        for k in range(near_count):
            hit = jnp.where(near_ref[k, t] == tile, 1, 0)
            listed = listed + hit
            which = which + hit * class_ref[0, k]
        scaled = taper_ref[which]
        if halves > 1:
            scaled = jnp.concatenate(
                [
                    scaled[:, who * owned + c * half : who * owned + (c + 1) * half]
                    for who in range(levels)
                ],
                axis=1,
            )
        scaled = scaled.astype(jnp.float32) / jnp.float32(members - 1)
        scaled = scaled * listed.astype(jnp.float32)
        covar = lax.dot_general(
            state_ref[...],
            y_buf[slot, c],
            (((1,), (1,)), ((), ())),
            preferred_element_type=jnp.float32,
        )
        tapered = (
            (covar.reshape(lev_dev, points, covar.shape[1]) * scaled[None])
            .reshape(covar.shape)
            .astype(jnp.bfloat16)
        )
        gain = jnp.dot(tapered, w_buf[slot, c], preferred_element_type=jnp.float32)
        out_ref[...] = gain if first else out_ref[...] + gain

    def relay_plane(a, h):
        send(a, rows(a, 1 + uneven, h), 3, h, jnp.where(uneven == 1, xn, yn))
        share(a, 1, h)
        share(a, 2, h)

    def spread(a, h):
        send(a, rows(a, 5 - odd_x, h), 6, h, xn)
        send(a, rows(a, 5 - odd_y, h), 7, h, yn)
        share(a, 4, h)
        share(a, 5, h)

    def relay_far(a, h):
        send(a, rows(a, relayed, h), 8, h, jnp.where(uneven == 1, yn, xn))
        share(a, relayed, h)

    def forward_plane(a, h):
        arrive(a, h, 1, 2)
        relay_plane(a, h)

    def forward_far(a, h):
        arrive(a, h, 4, 5)
        spread(a, h)

    def forward_relayed(a, h):
        arrive(a, h, relayed)
        relay_far(a, h)

    def settle(slot):
        def land(a, h):
            arrive(a, h, slot)
            share(a, slot, h)

        return land

    events = []
    for a, lead in ((W, 0), (Y, chunks)):
        for h in range(chunks):
            n = lead + h + 1
            events.append((n + 1, forward_plane, a, h))
            events.append((2 * n + 1.5, forward_far, a, h))
            far = max(2 * n + 3, 2 * chunks + 1.5 + n)
            events.append((far, forward_relayed, a, h))
            events.append((2 * chunks + 0.5 + n, settle(3), a, h))
            events.append((max(2 * n + 5, 2 * chunks + 8 + n), settle(final), a, h))
            events.append((max(2 * n + 5.1, 2 * chunks + 8.1 + n), settle(8), a, h))

    def keep(slot, c, at, first=False):
        events.append((at, lambda *_: compute(slot, c, first), None, None))

    for c in range(halves):
        n = chunks + (c + 1) * subs
        keep(0, c, 3.1 + 0.1 * c, c == 0)
        keep(1, c, n + 1.3)
        keep(2, c, n + 1.4)
        keep(4, c, 2 * n + 1.8)
        keep(5, c, 2 * n + 1.9)
        keep(3, c, 2 * chunks + 2.8 + n)
        keep(relayed, c, max(2 * n + 3, 2 * chunks + 1.5 + n) + 0.7)
        keep(final, c, max(2 * n + 5, 2 * chunks + 8 + n) + 0.2)
        keep(8, c, max(2 * n + 5, 2 * chunks + 8 + n) + 0.3)
    for _, act, a, h in sorted(events, key=lambda event: event[0]):
        act(a, h)
    for copy in started:
        copy.wait_send()


def shards(
    tiles, levels,
    anomalies, footprint, weighting, dual_rows, taper_blocks, obs_count, near_tiles, taper_class
):
    members, lev_dev, points = anomalies.shape
    owned = dual_rows.shape[0]
    cells = lev_dev * points
    halves = max(1, owned // points)
    chunks = halves * max(1, owned // halves // CHUNK)
    halves = max(1, owned // points)
    chunks = halves * max(1, owned // halves // CHUNK)
    state = anomalies.transpose(1, 2, 0).reshape(cells, members)
    smem = pl.BlockSpec(memory_space=pltpu.SMEM)
    vmem = pl.BlockSpec(memory_space=pltpu.VMEM)
    out = pl.pallas_call(
        functools.partial(kernel, tiles, levels, near_tiles.shape[1]),
        out_shape=jax.ShapeDtypeStruct((cells, members), jnp.float32),
        in_specs=[smem] * 3 + [vmem] * 5,
        out_specs=vmem,
        scratch_shapes=[
            pltpu.VMEM((cells, members), jnp.bfloat16),
            pltpu.VMEM((SLOTS, halves, levels * owned // halves, members), jnp.bfloat16),
            pltpu.VMEM((SLOTS, halves, levels * owned // halves, members), jnp.bfloat16),
            pltpu.VMEM((levels - 1, owned, members), jnp.float32),
            pltpu.VMEM((levels - 1, owned, members), jnp.float32),
            pltpu.SemaphoreType.DMA((2, SLOTS - 1, chunks)),
            pltpu.SemaphoreType.DMA((2, SLOTS - 1, chunks)),
            pltpu.SemaphoreType.DMA((2, SLOTS, chunks, levels - 1)),
            pltpu.SemaphoreType.DMA((2, SLOTS, chunks, levels - 1)),
            pltpu.SemaphoreType.DMA((levels - 1,)),
            pltpu.SemaphoreType.DMA((levels - 1,)),
        ],
        compiler_params=pltpu.CompilerParams(
            collective_id=0, has_side_effects=True, vmem_limit_bytes=48 * 1024 * 1024
        ),
    )(obs_count, near_tiles.T, taper_class, anomalies, footprint, weighting.T, dual_rows, taper_blocks)
    return out.T.reshape(members, lev_dev, points)


def solution(mesh):
    return jax.shard_map(
        functools.partial(shards, mesh.shape["tile"], mesh.shape["level"]),
        mesh=mesh,
        in_specs=(
            P(None, "level", "tile"),
            P("tile", None),
            P("level", "tile"),
            P(("tile", "level"), None),
            P(),
            P(),
            P(),
            P("tile", None),
        ),
        out_specs=P(None, "level", "tile"),
        check_vma=False,
    )
```

```python
import functools
import jax
import jax.numpy as jnp
from jax import lax
from jax.experimental import pallas as pl
from jax.experimental.pallas import tpu as pltpu
from jax.sharding import PartitionSpec as P

MESH = pl.DeviceIdType.MESH
PLANE = 4
SLOTS = 9
W, Y = 0, 1


def kernel(
    tiles, levels, near_count,
    counts_ref, near_ref, class_ref, state_ref, foot_ref, weight_ref, dual_ref, taper_ref,
    out_ref,
    w_buf, y_buf, sums, others, ici_send, ici_recv, sib_send, sib_recv, part_send, part_recv,
):
    t = lax.axis_index("tile")
    l = lax.axis_index("level")
    owned, members = dual_ref.shape
    chunks = w_buf.shape[1]
    chunk = owned // chunks
    cells = state_ref.shape[0]
    points = foot_ref.shape[1]
    lev_dev = cells // points
    p = lax.rem(t, PLANE)
    base = t - p
    odd_x = lax.rem(p, 2)
    odd_y = p // 2
    xn = t + 1 - 2 * odd_x
    yn = t + 2 - 4 * odd_y
    zp = lax.rem(t + PLANE, tiles)
    zm = lax.rem(t + tiles - PLANE, tiles)
    low = lax.rem(base + tiles - PLANE, tiles)
    high = lax.rem(base + PLANE, tiles)
    uneven = lax.rem(odd_x + odd_y, 2)
    bufs = (w_buf, y_buf)

    def sibling(k):
        return lax.rem(l + k, levels)

    barrier = pltpu.get_barrier_semaphore()
    for other in (xn, yn, zp, zm):
        pl.semaphore_signal(barrier, inc=1, device_id=(other, l), device_id_type=MESH)
    for k in range(1, levels):
        pl.semaphore_signal(barrier, inc=1, device_id=(t, sibling(k)), device_id_type=MESH)
    pl.semaphore_wait(barrier, 3 + levels)

    started = []

    def rows(a, slot, h):
        return bufs[a].at[slot, h, pl.ds(pl.multiple_of(l * chunk, chunk), chunk)]

    def hop(a, src, slot, h, to):
        return pltpu.make_async_remote_copy(
            src_ref=src,
            dst_ref=rows(a, slot, h),
            send_sem=ici_send.at[a, slot - 1, h],
            recv_sem=ici_recv.at[a, slot - 1, h],
            device_id=(to, l),
            device_id_type=MESH,
        )

    def send(a, src, slot, h, to):
        copy = hop(a, src, slot, h, to)
        copy.start()
        started.append(copy)

    def across(a, slot, h, k, src=None):
        return pltpu.make_async_remote_copy(
            src_ref=rows(a, slot, h) if src is None else src,
            dst_ref=rows(a, slot, h),
            send_sem=sib_send.at[a, slot, h, k - 1],
            recv_sem=sib_recv.at[a, slot, h, k - 1],
            device_id=(t, sibling(k)),
            device_id_type=MESH,
        )

    def share(a, slot, h, src=None):
        for k in range(1, levels):
            copy = across(a, slot, h, k, src)
            copy.start()
            started.append(copy)

    def arrive(a, h, *slots):
        for slot in slots:
            hop(a, rows(a, slot, h), slot, h, xn).wait_recv()

    def together(slot, h):
        for a in (W, Y):
            for k in range(1, levels):
                across(a, slot, h, k).wait_recv()

    def dual(h):
        return dual_ref.at[h * chunk : (h + 1) * chunk]

    for h in range(chunks):
        send(W, dual(h), 4, h, zp)
        send(W, dual(h), 5, h, zm)
        send(W, dual(h), 1, h, xn)
        send(W, dual(h), 2, h, yn)
    for h in range(chunks):
        share(W, 0, h, dual(h))

    def part(who):
        first = pl.multiple_of(who * owned, owned)
        feet = foot_ref[pl.ds(first, owned), :]
        total = None
        for j in range(lev_dev):
            seen = jnp.dot(
                feet,
                state_ref[j * points : (j + 1) * points, :],
                preferred_element_type=jnp.float32,
            )
            seen = weight_ref[pl.ds(first, owned), j : j + 1] * seen
            total = seen if total is None else total + seen
        return total

    parts = []
    for k in range(1, levels):
        sums[k - 1] = part(sibling(k))
        copy = pltpu.make_async_remote_copy(
            src_ref=sums.at[k - 1],
            dst_ref=others.at[k - 1],
            send_sem=part_send.at[k - 1],
            recv_sem=part_recv.at[k - 1],
            device_id=(t, sibling(k)),
            device_id_type=MESH,
        )
        copy.start()
        started.append(copy)
        parts.append(copy)
    observed = part(l)
    for k, copy in enumerate(parts):
        copy.wait_recv()
        observed = observed + others[k]
    slot_ids = l * owned + lax.broadcasted_iota(jnp.int32, observed.shape, 0)
    observed = jnp.where(slot_ids < counts_ref[t], observed, 0.0).astype(jnp.bfloat16)
    own = pl.ds(pl.multiple_of(l * chunk, chunk), chunk)
    for h in range(chunks):
        y_buf[0, h, own, :] = observed[h * chunk : (h + 1) * chunk]
    for h in range(chunks):
        send(Y, rows(Y, 0, h), 4, h, zp)
        send(Y, rows(Y, 0, h), 5, h, zm)
        send(Y, rows(Y, 0, h), 1, h, xn)
        send(Y, rows(Y, 0, h), 2, h, yn)
    for h in range(chunks):
        share(Y, 0, h)
        w_buf[0, h, own, :] = dual_ref[h * chunk : (h + 1) * chunk, :]

    def near_of(lower, position):
        return jnp.where(lower == 1, low, high) + position

    ahead_x = near_of(1 - odd_x, xn - base)
    ahead_y = near_of(1 - odd_y, yn - base)
    relayed, final = 7 - uneven, 6 + uneven
    tile_of = (
        (0, t), (1, xn), (2, yn), (3, base + PLANE - 1 - p), (4, zm), (5, zp),
        (relayed, jnp.where(uneven == 1, ahead_x, ahead_y)),
        (final, jnp.where(uneven == 1, ahead_y, ahead_x)),
        (8, near_of(1 - odd_y, PLANE - 1 - p)),
    )

    def compute(slot, h, first=False):
        together(slot, h)
        tile = [its for where, its in tile_of if where is slot][0]
        listed = jnp.int32(0)
        which = jnp.int32(0)
        for k in range(near_count):
            hit = jnp.where(near_ref[k, t] == tile, 1, 0)
            listed = listed + hit
            which = which + hit * class_ref[0, k]
        scaled = taper_ref[which]
        if chunks > 1:
            scaled = jnp.concatenate(
                [
                    scaled[:, who * owned + h * chunk : who * owned + (h + 1) * chunk]
                    for who in range(levels)
                ],
                axis=1,
            )
        scaled = scaled.astype(jnp.float32) / jnp.float32(members - 1)
        scaled = scaled * listed.astype(jnp.float32)
        covar = lax.dot_general(
            state_ref[...],
            y_buf[slot, h],
            (((1,), (1,)), ((), ())),
            preferred_element_type=jnp.float32,
        )
        tapered = (
            (covar.reshape(lev_dev, points, covar.shape[1]) * scaled[None])
            .reshape(covar.shape)
            .astype(jnp.bfloat16)
        )
        gain = jnp.dot(tapered, w_buf[slot, h], preferred_element_type=jnp.float32)
        out_ref[...] = gain if first else out_ref[...] + gain

    def relay_plane(a, h):
        send(a, rows(a, 1 + uneven, h), 3, h, jnp.where(uneven == 1, xn, yn))
        share(a, 1, h)
        share(a, 2, h)

    def spread(a, h):
        send(a, rows(a, 5 - odd_x, h), 6, h, xn)
        send(a, rows(a, 5 - odd_y, h), 7, h, yn)
        share(a, 4, h)
        share(a, 5, h)

    def relay_far(a, h):
        send(a, rows(a, relayed, h), 8, h, jnp.where(uneven == 1, yn, xn))
        share(a, relayed, h)

    every = range(chunks)
    last = chunks - 1
    arrive(W, 0, 1, 2)
    relay_plane(W, 0)
    compute(0, 0, True)
    arrive(W, 0, 4, 5)
    spread(W, 0)
    for h in range(1, chunks):
        arrive(W, h, 1, 2)
        relay_plane(W, h)
        compute(0, h)
    arrive(Y, 0, 1, 2)
    relay_plane(Y, 0)
    for h in range(1, chunks):
        arrive(W, h, 4, 5)
        spread(W, h)
        arrive(Y, h, 1, 2)
        relay_plane(Y, h)
    for h in every:
        compute(1, h)
        compute(2, h)
    arrive(W, 0, relayed)
    relay_far(W, 0)
    arrive(Y, 0, 4, 5)
    spread(Y, 0)
    for h in range(1, chunks):
        arrive(W, h, relayed)
        relay_far(W, h)
    compute(4, 0)
    compute(5, 0)
    for h in range(1, chunks):
        arrive(Y, h, 4, 5)
        spread(Y, h)
    arrive(Y, 0, relayed)
    relay_far(Y, 0)
    for h in range(1, chunks):
        compute(4, h)
        compute(5, h)
    for h in every:
        for a in (W, Y):
            arrive(a, h, 3)
            share(a, 3, h)
    compute(3, 0)
    compute(relayed, 0)
    for h in range(1, chunks):
        arrive(Y, h, relayed)
        relay_far(Y, h)
        compute(3, h)
    for h in every:
        arrive(W, h, final)
        share(W, final, h)
        arrive(W, h, 8)
        share(W, 8, h)
    for h in range(1, chunks):
        compute(relayed, h)
    for h in every:
        for slot in (final, 8):
            arrive(Y, h, slot)
            share(Y, slot, h)
            if h < last:
                compute(slot, h)
    compute(final, last)
    compute(8, last)
    for copy in started:
        copy.wait_send()


def shards(
    tiles, levels,
    anomalies, footprint, weighting, dual_rows, taper_blocks, obs_count, near_tiles, taper_class
):
    members, lev_dev, points = anomalies.shape
    owned = dual_rows.shape[0]
    cells = lev_dev * points
    chunks = 1
    state = anomalies.transpose(1, 2, 0).reshape(cells, members)
    smem = pl.BlockSpec(memory_space=pltpu.SMEM)
    vmem = pl.BlockSpec(memory_space=pltpu.VMEM)
    out = pl.pallas_call(
        functools.partial(kernel, tiles, levels, near_tiles.shape[1]),
        out_shape=jax.ShapeDtypeStruct((cells, members), jnp.float32),
        in_specs=[smem] * 3 + [vmem] * 5,
        out_specs=vmem,
        scratch_shapes=[
            pltpu.VMEM((SLOTS, chunks, levels * owned // chunks, members), jnp.bfloat16),
            pltpu.VMEM((SLOTS, chunks, levels * owned // chunks, members), jnp.bfloat16),
            pltpu.VMEM((levels - 1, owned, members), jnp.float32),
            pltpu.VMEM((levels - 1, owned, members), jnp.float32),
            pltpu.SemaphoreType.DMA((2, SLOTS - 1, chunks)),
            pltpu.SemaphoreType.DMA((2, SLOTS - 1, chunks)),
            pltpu.SemaphoreType.DMA((2, SLOTS, chunks, levels - 1)),
            pltpu.SemaphoreType.DMA((2, SLOTS, chunks, levels - 1)),
            pltpu.SemaphoreType.DMA((levels - 1,)),
            pltpu.SemaphoreType.DMA((levels - 1,)),
        ],
        compiler_params=pltpu.CompilerParams(
            collective_id=0, has_side_effects=True, vmem_limit_bytes=48 * 1024 * 1024
        ),
    )(obs_count, near_tiles.T, taper_class, state, footprint, weighting.T, dual_rows, taper_blocks)
    return out.T.reshape(members, lev_dev, points)


def solution(mesh):
    return jax.shard_map(
        functools.partial(shards, mesh.shape["tile"], mesh.shape["level"]),
        mesh=mesh,
        in_specs=(
            P(None, "level", "tile"),
            P("tile", None),
            P("level", "tile"),
            P(("tile", "level"), None),
            P(),
            P(),
            P(),
            P("tile", None),
        ),
        out_specs=P(None, "level", "tile"),
        check_vma=False,
    )
```
